32 devices in a mesh: tile: 16 (over z, x, core), wave: 2 (over y).
Axes of the slice: x: 2, y: 2, z: 4, core: 2. Of those that a mesh axis runs over, the one named last changes fastest.
Arguments:
- params: float32 [9, 256, 128], P(None, 'tile'), may hold values from -6 to 6
- dual_in: float32 [2, 9, 256, 128], P(None, None, 'tile'), may hold values from -4 to 4
- jacobian: bfloat16 [4, 9, 256, 128], P(None, None, 'tile'), may hold values from -3 to 3
- response: float32 [9, 64], P(None, 'wave'), may hold values from -5 to 5
- observed: bfloat16 [4, 64, 256, 128], P(None, 'wave', 'tile'), may hold values from -6 to 6
- psf: bfloat16 [17, 17], replicated, may hold values from -0.375 to 0.375
- step_size: float32 [], replicated, may hold values from 0.03 to 0.06
- dual_step: float32 [], replicated, may hold values from 0.5 to 1
- tv_bound: float32 [], replicated, may hold values from 1 to 2
- clip_bound: float32 [], replicated, may hold values from 0.5 to 1
Outputs:
- params_out: float32 [9, 256, 128], P(None, 'tile')
- dual_out: float32 [2, 9, 256, 128], P(None, None, 'tile')
- misfit: float32 [], replicated
The draws below stay inside these ranges and needn't reach their ends.
All inputs are finite; a program needn't handle non-finite values.
Results may differ from the reference program's by a relative error of at most 0.0033.
Values may be sent and summed in bfloat16 or wider, within the bound.
A program may use at most 128 MiB of HBM per device.

```python
import jax
import jax.numpy as jnp
from jax import lax

NCOL = 128
NPAR = 9
STOKES = 4
TAPS = 17
NROWS = 256
WAVE = 64


def block_levels(key, shape, shards, least, high):
    gain = 1.0
    for position, shards_of in shards:
        heights = jax.random.uniform(jax.random.fold_in(jax.random.fold_in(key, 6), position), (shards_of,), jnp.float32, least / len(shards), high / len(shards))
        gain = gain * jnp.repeat(jnp.exp(heights), shape[position] // shards_of).reshape((-1,) + (1,) * (len(shape) - 1 - position))
    return gain


def centred(own_key, dims, width, reach, pieces=(), kind=jnp.bfloat16):
    values = width * jax.random.normal(own_key, dims, jnp.float32)
    if pieces:
        values = values * block_levels(own_key, dims, pieces, -0.22, 0.18)
    return jnp.clip(values, -reach, reach).astype(kind)


def setup_inputs(seed: int = 0) -> dict:
    streams_of = jax.random.split(jax.random.key(seed), 11)
    params = centred(streams_of[0], (NPAR, NROWS, NCOL), 1.0, 6.0, ((1, 16),), jnp.float32)
    dual_in = centred(streams_of[1], (2, NPAR, NROWS, NCOL), 0.5, 4.0, ((2, 16),), jnp.float32)
    jacobian = centred(streams_of[2], (STOKES, NPAR, NROWS, NCOL), 0.35, 3.0, ((2, 16),))
    response = centred(streams_of[3], (NPAR, WAVE), 1.0, 5.0, ((1, 2),), jnp.float32)
    observed = centred(streams_of[4], (STOKES, WAVE, NROWS, NCOL), 1.0, 6.0, ((1, 2), (2, 16)))
    psf = centred(streams_of[5], (TAPS, TAPS), (TAPS * TAPS) ** -0.5, 0.375)
    step_size = jnp.clip(jax.random.uniform(streams_of[6], (), jnp.float32, 0.03, 0.06), 0.03, 0.06)
    dual_step = jnp.clip(jax.random.uniform(streams_of[7], (), jnp.float32, 0.5, 1.0), 0.5, 1.0)
    tv_bound = jnp.clip(jax.random.uniform(streams_of[8], (), jnp.float32, 1.0, 2.0), 1.0, 2.0)
    clip_bound = jnp.clip(jax.random.uniform(streams_of[9], (), jnp.float32, 0.5, 1.0), 0.5, 1.0)
    return dict(params=params, dual_in=dual_in, jacobian=jacobian, response=response, observed=observed, psf=psf, step_size=step_size, dual_step=dual_step, tv_bound=tv_bound, clip_bound=clip_bound)


def toeplitz(psf, ncol):
    rows = jnp.arange(ncol, dtype=jnp.int32)[:, None]
    cols = jnp.arange(ncol, dtype=jnp.int32)[None, :]
    offset = (rows - cols + 8) % ncol
    onehot = (offset[None] == jnp.arange(17, dtype=jnp.int32)[:, None, None]).astype(jnp.float32)
    mats = jnp.einsum('ab,bkj->akj', psf.astype(jnp.float32), onehot, precision=lax.Precision.HIGHEST)
    return mats.astype(jnp.bfloat16)


def blur_rows(padded, mats, adjoint):
    count = padded.shape[1] - 16
    total = jnp.zeros((padded.shape[0], count, padded.shape[2]), jnp.float32)
    for tap in range(17):
        window = padded[:, tap:tap + count].astype(jnp.float32)
        if adjoint:
            total = total + jnp.einsum('nrk,jk->nrj', window, mats[16 - tap].astype(jnp.float32), precision=lax.Precision.HIGHEST)
        else:
            total = total + jnp.einsum('nrk,kj->nrj', window, mats[tap].astype(jnp.float32), precision=lax.Precision.HIGHEST)
    return total


def wrap_rows(image):
    return jnp.concatenate([image[:, -8:], image, image[:, :8]], axis=1)


def reference(params, dual_in, jacobian, response, observed, psf, step_size, dual_step, tv_bound, clip_bound):
    mats = toeplitz(psf, params.shape[2])
    grad_r = jnp.roll(params, -1, axis=1) - params
    grad_c = jnp.roll(params, -1, axis=2) - params
    dual_out = jnp.clip(dual_in + dual_step * jnp.stack([grad_r, grad_c]), -tv_bound, tv_bound)
    divergence = (dual_out[0] - jnp.roll(dual_out[0], 1, axis=1)) + (dual_out[1] - jnp.roll(dual_out[1], 1, axis=2))

    def gradient(state):
        def per_stokes(pair):
            jac_one, obs_one = pair
            terms = jac_one.astype(jnp.float32) * state
            synthetic = jnp.einsum('pl,pij->lij', response, terms, precision=lax.Precision.HIGHEST).astype(jnp.bfloat16)
            blurred = blur_rows(wrap_rows(synthetic), mats, False)
            resid = blurred - obs_one.astype(jnp.float32)
            size = jnp.abs(resid)
            huber = jnp.sum(jnp.where(size <= clip_bound, 0.5 * resid * resid, clip_bound * size - 0.5 * clip_bound * clip_bound))
            weighted = jnp.clip(resid, -clip_bound, clip_bound).astype(jnp.bfloat16)
            back = blur_rows(wrap_rows(weighted), mats, True)
            along = jnp.einsum('pl,lij->pij', response, back, precision=lax.Precision.HIGHEST)
            return jac_one.astype(jnp.float32) * along, huber

        parts, hubers = lax.map(per_stokes, (jacobian, observed))
        return jnp.sum(parts, axis=0), jnp.sum(hubers)

    state = params
    misfit = jnp.float32(0.0)
    for step in range(2):
        grad_now, huber = gradient(state)
        if step == 0:
            misfit = huber / (observed.shape[0] * observed.shape[1] * observed.shape[2] * observed.shape[3])
        state = state - step_size * (grad_now - divergence)
    return state, dual_out, misfit
```

```python
import functools

import jax
import jax.numpy as jnp
from jax import lax
from jax.experimental import pallas as pl
from jax.experimental.pallas import tpu as pltpu
from jax.sharding import PartitionSpec as P

MESH = pl.DeviceIdType.MESH
HALO = 8
EDGE = 2 * HALO
TAPS = 17
PAIRS = 9
F32 = jnp.float32
BF16 = jnp.bfloat16


def split_hi_lo(value):
    high = value.astype(BF16).astype(F32)
    return high, value - high


def group_size(count):
    size = 1
    while size * size < count:
        size *= 2
    return size if count % size == 0 else count


def kernel(
    tiles, waves, total_count,
    params, dual, jac, obs, response, prow, step_size, dual_step, tv_bound, clip_bound,
    x_out, d_out, m_out,
    mats, obs_f, jac_f, terms, pairs, proj, acc, xpad, dpad, div, respad, rt, rbf, rtb,
    jac_up, jac_dn, par_up, par_dn, dual_up,
    contrib, wave_in, summed, edge_up, edge_dn,
    m_own, m_wave, m_group, m_cross,
    in_send, in_recv, w_send, w_recv, e_send, e_recv, mw_send, mw_recv,
    mg_send, mg_recv, mc_send, mc_recv,
):
    npar, rows, ncol = params.shape
    images = jac.shape[0]
    stokes = images // npar
    nwave = response.shape[1]
    nimg = stokes * nwave
    width = -(-images // 8) * 8
    padded = rows + EDGE
    npair = padded // 2
    opair = rows // 2
    me_t = lax.axis_index("tile")
    me_w = lax.axis_index("wave")
    up = lax.rem(me_t + tiles - 1, tiles)
    down = lax.rem(me_t + 1, tiles)
    gsize = group_size(tiles)
    ngroup = tiles // gsize
    my_group = me_t // gsize
    my_place = lax.rem(me_t, gsize)
    group_peers = [my_group * gsize + lax.rem(my_place + d, gsize) for d in range(1, gsize)]
    cross_peers = [lax.rem(my_group + d, ngroup) * gsize + my_place for d in range(1, ngroup)]
    wave_peers = [lax.rem(me_w + d, waves) for d in range(1, waves)]

    barrier = pltpu.get_barrier_semaphore()
    peers = [(t, me_w) for t in [up, down] + group_peers + cross_peers]
    peers += [(me_t, w) for w in wave_peers]
    for peer in peers:
        pl.semaphore_signal(barrier, inc=1, device_id=peer, device_id_type=MESH)
    pl.semaphore_wait(barrier, len(peers))

    def remote(src, dst, send, recv, peer):
        return pltpu.make_async_remote_copy(
            src_ref=src, dst_ref=dst, send_sem=send, recv_sem=recv,
            device_id=peer, device_id_type=MESH,
        )

    first = [
        remote(params.at[:, pl.ds(rows - HALO, HALO)], par_up, in_send.at[0], in_recv.at[0], (down, me_w)),
        remote(params.at[:, pl.ds(0, HALO)], par_dn, in_send.at[1], in_recv.at[1], (up, me_w)),
        remote(dual.at[0, :, pl.ds(rows - HALO, HALO)], dual_up, in_send.at[2], in_recv.at[2], (down, me_w)),
        remote(jac.at[:, pl.ds(rows - EDGE, EDGE)], jac_up, in_send.at[3], in_recv.at[3], (down, me_w)),
        remote(jac.at[:, pl.ds(0, EDGE)], jac_dn, in_send.at[4], in_recv.at[4], (up, me_w)),
    ]
    for copy in first:
        copy.start()

    step = step_size[0]
    clip = clip_bound[0]
    bound = tv_bound[0]
    dstep = dual_step[0]

    zero_block = jnp.zeros((ncol, ncol), BF16)
    mats[0, 0:ncol, ncol:] = zero_block
    mats[PAIRS - 1, ncol:, 0:ncol] = zero_block
    for tap in range(TAPS):
        base = jnp.broadcast_to(prow[tap:tap + 1, :], (ncol, ncol))
        block = pltpu.roll(base, 0, 1, stride=1, stride_axis=0).astype(BF16)
        if tap % 2 == 0:
            mats[tap // 2, 0:ncol, 0:ncol] = block
            mats[tap // 2, ncol:, ncol:] = block
        else:
            mats[tap // 2, ncol:, 0:ncol] = block
            mats[tap // 2 + 1, 0:ncol, ncol:] = block

    respad[...] = jnp.zeros_like(respad)
    respad[0:npar, 0:nwave] = response[...]
    rt[...] = jnp.zeros_like(rt)
    spread = respad[...]
    for s in range(stokes):
        shifted = spread if s == 0 else pltpu.roll(spread, s * nwave, 1)
        for part in range(3):
            at = part * width + s * npar
            rt[at:at + npar, :] = shifted[0:npar]
    full = rt[...]
    high, low = split_hi_lo(full)
    place = lax.broadcasted_iota(jnp.int32, full.shape, 0)
    rbf[...] = jnp.where(place < 2 * width, high, low).T.astype(BF16)
    rtb[...] = jnp.concatenate([high[0:width], low[0:width]], axis=0).astype(BF16)

    obs_f[...] = obs[...].astype(F32).reshape(nimg * rows, ncol)
    for m in range(images):
        jac_f[m, HALO:HALO + rows, :] = jac[m].astype(F32)
    for m in range(images, width):
        terms[m * padded:(m + 1) * padded, :] = jnp.zeros((padded, ncol), F32)
    d1 = params[...]
    d1 = pltpu.roll(d1, ncol - 1, 2) - d1
    d1 = jnp.clip(dual[1] + dstep * d1, -bound, bound)
    d_out[1] = d1
    xpad[:, HALO:HALO + rows, :] = params[...]

    for copy in first:
        copy.wait()
    xpad[:, 0:HALO, :] = par_up[...]
    xpad[:, HALO + rows:, :] = par_dn[...]
    for m in range(images):
        jac_f[m, 0:HALO, :] = jac_up[m].astype(F32)[HALO:]
        jac_f[m, HALO + rows:, :] = jac_dn[m].astype(F32)[:HALO]
    d0 = xpad[:, HALO + 1:HALO + 1 + rows, :] - xpad[:, HALO:HALO + rows, :]
    d0 = jnp.clip(dual[0] + dstep * d0, -bound, bound)
    d_out[0] = d0
    edge = xpad[:, 1:HALO + 1, :] - xpad[:, 0:HALO, :]
    dpad[:, 0:HALO, :] = jnp.clip(dual_up[...] + dstep * edge, -bound, bound)
    dpad[:, HALO:, :] = d0
    div[...] = (d0 - dpad[:, HALO - 1:HALO - 1 + rows, :]) + (d1 - pltpu.roll(d1, 1, 2))

    zero_k = jnp.zeros((rbf.shape[1] - 3 * width, 2 * ncol), F32)
    own_first = me_w == 0

    for it in range(2):
        for m in range(images):
            terms[m * padded:(m + 1) * padded, :] = jac_f[m] * xpad[m % npar]
        for q in range(npair):
            for i in range(2):
                value = terms[pl.ds(2 * q + i, width, stride=padded), :]
                value = jnp.concatenate(split_hi_lo(value), axis=0).astype(BF16)
                pairs[q * 2 * width:(q + 1) * 2 * width, i * ncol:(i + 1) * ncol] = value
        total = None
        for k in range(PAIRS):
            window = pairs[k * 2 * width:(k + opair) * 2 * width, :]
            part = jnp.dot(window, mats[k], preferred_element_type=F32)
            total = part if total is None else total + part
        loss = jnp.zeros((8, ncol), F32)
        for r in range(opair):
            both = total[r * 2 * width:(r + 1) * 2 * width]
            bhi, blo = split_hi_lo(both[:width] + both[width:])
            stack = jnp.concatenate([bhi, blo, bhi, zero_k], axis=0).astype(BF16)
            blurred = jnp.dot(rbf[...], stack, preferred_element_type=F32)
            halves = []
            for i in range(2):
                target = obs_f[pl.ds(2 * r + i, nimg, stride=rows), :]
                resid = blurred[:, i * ncol:(i + 1) * ncol] - target
                held = jnp.clip(resid, -clip, clip)
                if it == 0:
                    huber = held * (resid - 0.5 * held)
                    loss = loss + jnp.sum(huber.reshape(nimg // 8, 8, ncol), axis=0)
                halves.append(held.astype(BF16))
            weighted = jnp.concatenate(halves, axis=1)
            both = jnp.dot(rtb[...], weighted, preferred_element_type=F32)
            value = jnp.concatenate(split_hi_lo(both[:width] + both[width:]), axis=0)
            proj[r * 2 * width:(r + 1) * 2 * width, :] = value.astype(BF16)
        copies_m = []
        if it == 0:
            m_own[...] = loss
            m_wave[me_w] = loss
            for d, w in enumerate(wave_peers):
                copies_m.append(remote(m_own, m_wave.at[me_w], mw_send.at[d], mw_recv.at[d], (me_t, w)))
            for copy in copies_m:
                copy.start()
        for k in range(PAIRS):
            back = lax.dot_general(
                proj[...], mats[k], (((1,), (1,)), ((), ())), preferred_element_type=F32
            )
            for q in range(opair):
                both = back[q * 2 * width:(q + 1) * 2 * width]
                both = both[:width] + both[width:]
                at = (k + q) * width
                if k == 0 or q == opair - 1:
                    acc[at:at + width, :] = both
                else:
                    acc[at:at + width, :] += both
        for q in range(npair):
            for i in range(2):
                value = acc[q * width:(q + 1) * width, i * ncol:(i + 1) * ncol]
                terms[pl.ds(2 * q + i, width, stride=padded), :] = value
        for p in range(npar):
            grad = None
            for s in range(stokes):
                m = s * npar + p
                part = jac_f[m] * terms[m * padded:(m + 1) * padded, :]
                grad = part if grad is None else grad + part
            grad = grad * (-step)
            centre = xpad[p, HALO:HALO + rows, :] + step * div[p]
            centre = jnp.where(own_first, centre, jnp.zeros_like(centre))
            value = jnp.concatenate(
                [grad[:HALO], grad[HALO:HALO + rows] + centre, grad[HALO + rows:]], axis=0
            )
            contrib[it, p] = value
            wave_in[it, me_w, p] = value
        copies_w = [
            remote(contrib.at[it], wave_in.at[it, me_w], w_send.at[it, d], w_recv.at[it, d], (me_t, w))
            for d, w in enumerate(wave_peers)
        ]
        for copy in copies_w:
            copy.start()
        if it == 1:
            mid = m_group[0]
            for g in range(1, gsize):
                mid = mid + m_group[g]
            m_own[...] = mid
            m_cross[my_group] = mid
            copies_c = [
                remote(m_own, m_cross.at[my_group], mc_send.at[d], mc_recv.at[d], (t, me_w))
                for d, t in enumerate(cross_peers)
            ]
            for copy in copies_c:
                copy.start()
        for copy in copies_w + copies_m:
            copy.wait()
        whole = wave_in[it, 0]
        for w in range(1, waves):
            whole = whole + wave_in[it, w]
        summed[it] = whole
        reach = EDGE if it == 0 else HALO
        copies_e = [
            remote(summed.at[it, :, pl.ds(0, reach)], edge_dn.at[it, :, pl.ds(0, reach)],
                   e_send.at[it, 0], e_recv.at[it, 0], (up, me_w)),
            remote(summed.at[it, :, pl.ds(padded - reach, reach)], edge_up.at[it, :, pl.ds(0, reach)],
                   e_send.at[it, 1], e_recv.at[it, 1], (down, me_w)),
        ]
        for copy in copies_e:
            copy.start()
        if it == 0:
            mid = m_wave[0]
            for w in range(1, waves):
                mid = mid + m_wave[w]
            m_own[...] = mid
            m_group[my_place] = mid
            copies_g = [
                remote(m_own, m_group.at[my_place], mg_send.at[d], mg_recv.at[d], (t, me_w))
                for d, t in enumerate(group_peers)
            ]
            for copy in copies_g:
                copy.start()
            for copy in copies_e + copies_g:
                copy.wait()
            xpad[:, 0:EDGE, :] = summed[0, :, 0:EDGE, :] + edge_up[0]
            if rows > EDGE:
                xpad[:, EDGE:rows, :] = summed[0, :, EDGE:rows, :]
            xpad[:, rows:, :] = summed[0, :, rows:, :] + edge_dn[0]
        else:
            for copy in copies_e + copies_c:
                copy.wait()
            x_out[:, 0:HALO, :] = summed[1, :, HALO:EDGE, :] + edge_up[1, :, 0:HALO, :]
            if rows > EDGE:
                x_out[:, HALO:rows - HALO, :] = summed[1, :, EDGE:rows, :]
            x_out[:, rows - HALO:, :] = summed[1, :, rows:rows + HALO, :] + edge_dn[1, :, 0:HALO, :]
            tot = m_cross[0]
            for g in range(1, ngroup):
                tot = tot + m_cross[g]
            m_out[0] = jnp.sum(tot) / total_count


def per_device(
    params, dual_in, jacobian, response, observed, psf, step_size, dual_step, tv_bound, clip_bound
):
    stokes, nwave, rows, ncol = observed.shape
    npar = params.shape[0]
    nimg = stokes * nwave
    images = stokes * npar
    width = -(-images // 8) * 8
    kdim = -(-3 * width // 128) * 128
    padded = rows + EDGE
    npair = padded // 2
    opair = rows // 2
    tiles = lax.axis_size("tile")
    waves = lax.axis_size("wave")
    total_count = float(nimg * waves * rows * tiles * ncol)
    gsize = group_size(tiles)
    ngroup = tiles // gsize
    flipped = psf[:, ::-1].astype(F32)
    prow = jnp.concatenate(
        [flipped[:, HALO:], jnp.zeros((TAPS, ncol - TAPS), F32), flipped[:, :HALO]], axis=1
    )
    vmem = pl.BlockSpec(memory_space=pltpu.VMEM)
    smem = pl.BlockSpec(memory_space=pltpu.SMEM)
    dma = pltpu.SemaphoreType.DMA
    state, dual_out, misfit = pl.pallas_call(
        functools.partial(kernel, tiles, waves, total_count),
        out_shape=(
            jax.ShapeDtypeStruct((npar, rows, ncol), F32),
            jax.ShapeDtypeStruct((2, npar, rows, ncol), F32),
            jax.ShapeDtypeStruct((1,), F32),
        ),
        in_specs=[vmem] * 6 + [smem] * 4,
        out_specs=(vmem, vmem, smem),
        scratch_shapes=[
            pltpu.VMEM((PAIRS, 2 * ncol, 2 * ncol), BF16),
            pltpu.VMEM((nimg * rows, ncol), F32),
            pltpu.VMEM((images, padded, ncol), F32),
            pltpu.VMEM((width * padded, ncol), F32),
            pltpu.VMEM((npair * 2 * width, 2 * ncol), BF16),
            pltpu.VMEM((opair * 2 * width, 2 * ncol), BF16),
            pltpu.VMEM((npair * width, 2 * ncol), F32),
            pltpu.VMEM((npar, padded, ncol), F32),
            pltpu.VMEM((npar, rows + HALO, ncol), F32),
            pltpu.VMEM((npar, rows, ncol), F32),
            pltpu.VMEM((-(-npar // 8) * 8, nimg), F32),
            pltpu.VMEM((kdim, nimg), F32),
            pltpu.VMEM((nimg, kdim), BF16),
            pltpu.VMEM((2 * width, nimg), BF16),
            pltpu.VMEM((images, EDGE, ncol), BF16),
            pltpu.VMEM((images, EDGE, ncol), BF16),
            pltpu.VMEM((npar, HALO, ncol), F32),
            pltpu.VMEM((npar, HALO, ncol), F32),
            pltpu.VMEM((npar, HALO, ncol), F32),
            pltpu.VMEM((2, npar, padded, ncol), F32),
            pltpu.VMEM((2, waves, npar, padded, ncol), F32),
            pltpu.VMEM((2, npar, padded, ncol), F32),
            pltpu.VMEM((2, npar, EDGE, ncol), F32),
            pltpu.VMEM((2, npar, EDGE, ncol), F32),
            pltpu.VMEM((8, ncol), F32),
            pltpu.VMEM((waves, 8, ncol), F32),
            pltpu.VMEM((gsize, 8, ncol), F32),
            pltpu.VMEM((ngroup, 8, ncol), F32),
            dma((5,)), dma((5,)),
            dma((2, max(waves - 1, 1))), dma((2, max(waves - 1, 1))),
            dma((2, 2)), dma((2, 2)),
            dma((max(waves - 1, 1),)), dma((max(waves - 1, 1),)),
            dma((max(gsize - 1, 1),)), dma((max(gsize - 1, 1),)),
            dma((max(ngroup - 1, 1),)), dma((max(ngroup - 1, 1),)),
        ],
        compiler_params=pltpu.CompilerParams(
            collective_id=0, has_side_effects=True, vmem_limit_bytes=48 * 1024 * 1024
        ),
    )(
        params, dual_in, jacobian.reshape(images, rows, ncol),
        observed.reshape(nimg, rows, ncol), response, prow,
        step_size.reshape(1), dual_step.reshape(1), tv_bound.reshape(1), clip_bound.reshape(1),
    )
    return state, dual_out, misfit.reshape(())


def solution(mesh):
    in_specs = (
        P(None, "tile", None),
        P(None, None, "tile", None),
        P(None, None, "tile", None),
        P(None, "wave"),
        P(None, "wave", "tile", None),
        P(),
        P(),
        P(),
        P(),
        P(),
    )
    out_specs = (P(None, "tile", None), P(None, None, "tile", None), P())
    return jax.shard_map(
        per_device, mesh=mesh, in_specs=in_specs, out_specs=out_specs, check_vma=False
    )
```

```python
import functools

import jax
import jax.numpy as jnp
from jax import lax
from jax.experimental import pallas as pl
from jax.experimental.pallas import tpu as pltpu
from jax.sharding import PartitionSpec as P

MESH = pl.DeviceIdType.MESH
HALO = 8
EDGE = 2 * HALO
TAPS = 17
PAIRS = 9
F32 = jnp.float32
BF16 = jnp.bfloat16


def split_hi_lo(value):
    high = value.astype(BF16).astype(F32)
    return high, value - high


def group_size(count):
    size = 1
    while size * size < count:
        size *= 2
    return size if count % size == 0 else count


def kernel(
    tiles, waves, total_count,
    params_h, dual_h, jac_h, obs_h, response, psf, step_size, dual_step, tv_bound, clip_bound,
    x_out, d_out, m_out,
    params, dual, jac, obs,
    mats, obs_f, jac_f, terms, pairs, proj, acc, xpad, dpad, base, respad, psfpad, rt, rbf, rtb,
    jac_edge, jac_up, jac_dn, par_up, par_dn, dual_up, div_edge, div_up, div_dn,
    full0, edge0, full1, edge1, full0_in, up0_in, dn0_in, full1_in, up1_in, dn1_in,
    m_own, m_mid, m_group, m_cross,
    local, in_send, in_recv, f_send, f_recv, u_send, u_recv, d_send, d_recv,
    mg_send, mg_recv, mc_send, mc_recv,
):
    npar, rows, ncol = params.shape
    images = jac.shape[0]
    stokes = images // npar
    nwave = response.shape[1]
    nimg = stokes * nwave
    width = -(-images // 8) * 8
    wide = -(-images // 16) * 16
    padded = rows + EDGE
    npair = padded // 2
    opair = rows // 2
    me_t = lax.axis_index("tile")
    me_w = lax.axis_index("wave")
    up = lax.rem(me_t + tiles - 1, tiles)
    down = lax.rem(me_t + 1, tiles)
    gsize = group_size(tiles)
    ngroup = tiles // gsize
    my_group = me_t // gsize
    my_place = lax.rem(me_t, gsize)
    spin = [me_w] + [lax.rem(me_w + d, waves) for d in range(1, waves)]
    group_tiles = [me_t]
    group_tiles += [my_group * gsize + lax.rem(my_place + d, gsize) for d in range(1, gsize)]
    group_peers = [(t, w) for i, t in enumerate(group_tiles) for j, w in enumerate(spin) if i + j > 0]
    cross_peers = [
        (lax.rem(my_group + d, ngroup) * gsize + my_place, me_w) for d in range(1, ngroup)
    ]

    barrier = pltpu.get_barrier_semaphore()
    peers = [(t, w) for w in spin for t in (up, down)] + group_peers + cross_peers
    for peer in peers:
        pl.semaphore_signal(barrier, inc=1, device_id=peer, device_id_type=MESH)
    fetch = [
        pltpu.make_async_copy(jac_h, jac, local.at[0]),
        pltpu.make_async_copy(params_h, params, local.at[1]),
        pltpu.make_async_copy(dual_h, dual, local.at[2]),
        pltpu.make_async_copy(obs_h, obs, local.at[3]),
    ]
    for copy in fetch:
        copy.start()
    fetch[0].wait()
    for m in range(images):
        jac_f[m, HALO:HALO + rows, :] = jac[m].astype(F32)
    jac_edge[0] = jac_f[:, HALO:EDGE, :].reshape(images * HALO, ncol).astype(BF16)
    jac_edge[1] = jac_f[:, rows:rows + HALO, :].reshape(images * HALO, ncol).astype(BF16)
    fetch[1].wait()
    fetch[2].wait()
    pl.semaphore_wait(barrier, len(peers))

    def remote(src, dst, send, recv, peer):
        return pltpu.make_async_remote_copy(
            src_ref=src, dst_ref=dst, send_sem=send, recv_sem=recv,
            device_id=peer, device_id_type=MESH,
        )

    above, below = (up, me_w), (down, me_w)
    first = [
        remote(params.at[:, pl.ds(rows - HALO, HALO)], par_up, in_send.at[0], in_recv.at[0], below),
        remote(params.at[:, pl.ds(0, HALO)], par_dn, in_send.at[1], in_recv.at[1], above),
        remote(dual.at[0, :, pl.ds(rows - HALO, HALO)], dual_up, in_send.at[2], in_recv.at[2], below),
        remote(jac_edge.at[1], jac_up, in_send.at[3], in_recv.at[3], below),
        remote(jac_edge.at[0], jac_dn, in_send.at[4], in_recv.at[4], above),
    ]
    for copy in first:
        copy.start()

    step = step_size[0]
    clip = clip_bound[0]
    bound = tv_bound[0]
    dstep = dual_step[0]

    zero_block = jnp.zeros((ncol, ncol), BF16)
    mats[0, ncol:, 0:ncol] = zero_block
    mats[PAIRS - 1, 0:ncol, ncol:] = zero_block
    psfpad[...] = jnp.zeros_like(psfpad)
    psfpad[0:TAPS, 0:TAPS] = psf[...].astype(F32)
    taps = pltpu.roll(psfpad[...], ncol - HALO, 1)
    for tap in range(TAPS):
        line = jnp.broadcast_to(taps[tap:tap + 1, :], (ncol, ncol))
        block = pltpu.roll(line, 0, 1, stride=1, stride_axis=0).astype(BF16)
        if tap % 2 == 0:
            mats[tap // 2, 0:ncol, 0:ncol] = block
            mats[tap // 2, ncol:, ncol:] = block
        else:
            mats[tap // 2, 0:ncol, ncol:] = block
            mats[tap // 2 + 1, ncol:, 0:ncol] = block

    respad[...] = jnp.zeros_like(respad)
    respad[0:npar, 0:nwave] = response[...]
    rt[...] = jnp.zeros_like(rt)
    spread = respad[...]
    for s in range(stokes):
        shifted = spread if s == 0 else pltpu.roll(spread, s * nwave, 1)
        for part in range(3):
            at = part * width + s * npar
            rt[at:at + npar, :] = shifted[0:npar]
    full = rt[...]
    high, low = split_hi_lo(full)
    place = lax.broadcasted_iota(jnp.int32, full.shape, 0)
    rbf[...] = jnp.where(place < 2 * width, high, low).T.astype(BF16)
    rtb[...] = jnp.concatenate([high[0:width], low[0:width]], axis=0).astype(BF16)

    for m in range(images, width):
        terms[m * padded:(m + 1) * padded, :] = jnp.zeros((padded, ncol), F32)
    d1 = params[...]
    xpad[:, HALO:HALO + rows, :] = d1
    d1 = pltpu.roll(d1, ncol - 1, 2) - d1
    d1 = jnp.clip(dual[1] + dstep * d1, -bound, bound)
    d_out[1] = d1
    fetch[3].wait()
    obs_f[...] = obs[...].astype(F32).reshape(nimg * rows, ncol)

    for copy in first:
        copy.wait()
    xpad[:, 0:HALO, :] = par_up[...]
    xpad[:, HALO + rows:, :] = par_dn[...]
    d0 = xpad[:, HALO + 1:HALO + 1 + rows, :] - xpad[:, HALO:HALO + rows, :]
    d0 = jnp.clip(dual[0] + dstep * d0, -bound, bound)
    d_out[0] = d0
    side = xpad[:, 1:HALO + 1, :] - xpad[:, 0:HALO, :]
    dpad[:, 0:HALO, :] = jnp.clip(dual_up[...] + dstep * side, -bound, bound)
    dpad[:, HALO:, :] = d0
    div = (d0 - dpad[:, HALO - 1:HALO - 1 + rows, :]) + (d1 - pltpu.roll(d1, 1, 2))
    base[:, HALO:HALO + rows, :] = div
    div_edge[0] = div[:, 0:HALO, :]
    div_edge[1] = div[:, rows - HALO:, :]
    copies_v = [
        remote(div_edge.at[1], div_up, in_send.at[5], in_recv.at[5], below),
        remote(div_edge.at[0], div_dn, in_send.at[6], in_recv.at[6], above),
    ]
    for copy in copies_v:
        copy.start()
    jac_f[:, 0:HALO, :] = jac_up[...].astype(F32).reshape(images, HALO, ncol)
    jac_f[:, HALO + rows:, :] = jac_dn[...].astype(F32).reshape(images, HALO, ncol)

    zero_k = jnp.zeros((rbf.shape[1] - 3 * width, 2 * ncol), F32)

    def widen(value):
        if wide == width:
            return value.astype(BF16)
        fill = jnp.zeros((wide - width, value.shape[1]), F32)
        return jnp.concatenate([value, fill], axis=0).astype(BF16)

    for it in range(2):
        for m in range(images):
            terms[m * padded:(m + 1) * padded, :] = jac_f[m] * xpad[m % npar]
        for q in range(npair):
            for i in range(2):
                value = terms[pl.ds(2 * q + i, width, stride=padded), :]
                pairs[q * wide:(q + 1) * wide, i * ncol:(i + 1) * ncol] = widen(value)
        total = None
        for k in range(PAIRS):
            window = pairs[k * wide:(k + opair) * wide, :]
            part = lax.dot_general(
                window, mats[k], (((1,), (1,)), ((), ())), preferred_element_type=F32
            )
            total = part if total is None else total + part
        loss = jnp.zeros((8, ncol), F32)
        for r in range(opair):
            bhi, blo = split_hi_lo(total[r * wide:r * wide + width])
            stack = jnp.concatenate([bhi, blo, bhi, zero_k], axis=0).astype(BF16)
            blurred = jnp.dot(rbf[...], stack, preferred_element_type=F32)
            halves = []
            for i in range(2):
                target = obs_f[pl.ds(2 * r + i, nimg, stride=rows), :]
                resid = blurred[:, i * ncol:(i + 1) * ncol] - target
                held = jnp.clip(resid, -clip, clip)
                if it == 0:
                    huber = held * (resid - 0.5 * held)
                    loss = loss + jnp.sum(huber.reshape(nimg // 8, 8, ncol), axis=0)
                halves.append(held.astype(BF16))
            weighted = jnp.concatenate(halves, axis=1)
            both = jnp.dot(rtb[...], weighted, preferred_element_type=F32)
            proj[r * wide:(r + 1) * wide, :] = widen(both[:width] + both[width:])
        if it == 0:
            m_own[...] = loss
            slot = my_place * waves + me_w
            m_group[slot] = loss
            copies_g = [
                remote(m_own, m_group.at[slot], mg_send.at[d], mg_recv.at[d], peer)
                for d, peer in enumerate(group_peers)
            ]
            for copy in copies_g:
                copy.start()
        for k in range(PAIRS):
            back = jnp.dot(proj[...], mats[k], preferred_element_type=F32)
            for q in range(opair):
                part = back[q * wide:(q + 1) * wide]
                at = (k + q) * wide
                if k == 0 or q == opair - 1:
                    acc[at:at + wide, :] = part
                else:
                    acc[at:at + wide, :] += part
        for q in range(npair):
            for i in range(2):
                value = acc[q * wide:q * wide + width, i * ncol:(i + 1) * ncol]
                terms[pl.ds(2 * q + i, width, stride=padded), :] = value
        grads = []
        for p in range(npar):
            grad = None
            for s in range(stokes):
                m = s * npar + p
                part = jac_f[m] * terms[m * padded:(m + 1) * padded, :]
                grad = part if grad is None else grad + part
            grads.append(grad)
        reach = EDGE if it == 0 else HALO
        whole = grads if it == 0 else [g[HALO:HALO + rows] for g in grads]
        whole = jnp.concatenate(whole, axis=0).astype(BF16)
        full_out, edge_out = (full0, edge0) if it == 0 else (full1, edge1)
        full_in, up_in, dn_in = (full0_in, up0_in, dn0_in) if it == 0 else (full1_in, up1_in, dn1_in)
        edge_out[0] = jnp.concatenate([g[:reach] for g in grads], axis=0).astype(BF16)
        edge_out[1] = jnp.concatenate([g[padded - reach:] for g in grads], axis=0).astype(BF16)
        full_out[...] = whole
        full_in[me_w] = whole
        copies = []
        for d in range(waves - 1, -1, -1):
            copies += [
                remote(edge_out.at[1], up_in.at[me_w], u_send.at[it, d], u_recv.at[it, d], (down, spin[d])),
                remote(edge_out.at[0], dn_in.at[me_w], d_send.at[it, d], d_recv.at[it, d], (up, spin[d])),
            ]
        for d in range(1, waves):
            copies.append(
                remote(full_out, full_in.at[me_w], f_send.at[it, d], f_recv.at[it, d], (me_t, spin[d]))
            )
        for copy in copies:
            copy.start()
        if it == 0:
            for copy in copies_v:
                copy.wait()
            base[:, 0:HALO, :] = div_up[...]
            base[:, HALO + rows:, :] = div_dn[...]
            base[...] = xpad[...] + step * base[...]
        for copy in copies:
            copy.wait()

        def added(ref, count):
            value = ref[0].astype(F32)
            for w in range(1, waves):
                value = value + ref[w].astype(F32)
            return value.reshape(npar, count, ncol)

        span = padded if it == 0 else rows
        inner = added(full_in, span)
        top = inner[:, :reach] + added(up_in, reach)
        low = inner[:, span - reach:] + added(dn_in, reach)
        if it == 0:
            kept = [base[:, :reach, :] - step * top]
            if span > 2 * reach:
                kept.append(base[:, reach:span - reach, :] - step * inner[:, reach:span - reach])
            kept.append(base[:, span - reach:, :] - step * low)
            mid = base[:, HALO:HALO + rows, :] - xpad[:, HALO:HALO + rows, :]
            at = 0
            for value in kept:
                xpad[:, at:at + value.shape[1], :] = value
                at += value.shape[1]
            base[:, HALO:HALO + rows, :] = xpad[:, HALO:HALO + rows, :] + mid
            for copy in copies_g:
                copy.wait()
            total_m = m_group[0]
            for g in range(1, gsize * waves):
                total_m = total_m + m_group[g]
            m_mid[...] = total_m
            m_cross[my_group] = total_m
            copies_c = [
                remote(m_mid, m_cross.at[my_group], mc_send.at[d], mc_recv.at[d], peer)
                for d, peer in enumerate(cross_peers)
            ]
            for copy in copies_c:
                copy.start()
        else:
            x_out[:, 0:reach, :] = base[:, HALO:HALO + reach, :] - step * top
            if span > 2 * reach:
                x_out[:, reach:span - reach, :] = (
                    base[:, HALO + reach:HALO + span - reach, :] - step * inner[:, reach:span - reach]
                )
            x_out[:, span - reach:, :] = base[:, HALO + span - reach:HALO + span, :] - step * low
            for copy in copies_c:
                copy.wait()
            tot = m_cross[0]
            for g in range(1, ngroup):
                tot = tot + m_cross[g]
            m_out[0] = jnp.sum(tot) / total_count


def per_device(
    params, dual_in, jacobian, response, observed, psf, step_size, dual_step, tv_bound, clip_bound
):
    stokes, nwave, rows, ncol = observed.shape
    npar = params.shape[0]
    nimg = stokes * nwave
    images = stokes * npar
    width = -(-images // 8) * 8
    wide = -(-images // 16) * 16
    kdim = -(-3 * width // 128) * 128
    padded = rows + EDGE
    npair = padded // 2
    opair = rows // 2
    tiles = lax.axis_size("tile")
    waves = lax.axis_size("wave")
    total_count = float(nimg * waves * rows * tiles * ncol)
    gsize = group_size(tiles)
    ngroup = tiles // gsize
    vmem = pl.BlockSpec(memory_space=pltpu.VMEM)
    smem = pl.BlockSpec(memory_space=pltpu.SMEM)
    hbm = pl.BlockSpec(memory_space=pltpu.HBM)
    dma = pltpu.SemaphoreType.DMA
    state, dual_out, misfit = pl.pallas_call(
        functools.partial(kernel, tiles, waves, total_count),
        out_shape=(
            jax.ShapeDtypeStruct((npar, rows, ncol), F32),
            jax.ShapeDtypeStruct((2, npar, rows, ncol), F32),
            jax.ShapeDtypeStruct((1,), F32),
        ),
        in_specs=[hbm] * 4 + [vmem] * 2 + [smem] * 4,
        out_specs=(vmem, vmem, smem),
        scratch_shapes=[
            pltpu.VMEM((npar, rows, ncol), F32),
            pltpu.VMEM((2, npar, rows, ncol), F32),
            pltpu.VMEM((images, rows, ncol), BF16),
            pltpu.VMEM((nimg, rows, ncol), BF16),
            pltpu.VMEM((PAIRS, 2 * ncol, 2 * ncol), BF16),
            pltpu.VMEM((nimg * rows, ncol), F32),
            pltpu.VMEM((images, padded, ncol), F32),
            pltpu.VMEM((width * padded, ncol), F32),
            pltpu.VMEM((npair * wide, 2 * ncol), BF16),
            pltpu.VMEM((opair * wide, 2 * ncol), BF16),
            pltpu.VMEM((npair * wide, 2 * ncol), F32),
            pltpu.VMEM((npar, padded, ncol), F32),
            pltpu.VMEM((npar, rows + HALO, ncol), F32),
            pltpu.VMEM((npar, padded, ncol), F32),
            pltpu.VMEM((-(-npar // 8) * 8, nimg), F32),
            pltpu.VMEM((-(-TAPS // 8) * 8, ncol), F32),
            pltpu.VMEM((kdim, nimg), F32),
            pltpu.VMEM((nimg, kdim), BF16),
            pltpu.VMEM((2 * width, nimg), BF16),
            pltpu.VMEM((2, images * HALO, ncol), BF16),
            pltpu.VMEM((images * HALO, ncol), BF16),
            pltpu.VMEM((images * HALO, ncol), BF16),
            pltpu.VMEM((npar, HALO, ncol), F32),
            pltpu.VMEM((npar, HALO, ncol), F32),
            pltpu.VMEM((npar, HALO, ncol), F32),
            pltpu.VMEM((2, npar, HALO, ncol), F32),
            pltpu.VMEM((npar, HALO, ncol), F32),
            pltpu.VMEM((npar, HALO, ncol), F32),
            pltpu.VMEM((npar * padded, ncol), BF16),
            pltpu.VMEM((2, npar * EDGE, ncol), BF16),
            pltpu.VMEM((npar * rows, ncol), BF16),
            pltpu.VMEM((2, npar * HALO, ncol), BF16),
            pltpu.VMEM((waves, npar * padded, ncol), BF16),
            pltpu.VMEM((waves, npar * EDGE, ncol), BF16),
            pltpu.VMEM((waves, npar * EDGE, ncol), BF16),
            pltpu.VMEM((waves, npar * rows, ncol), BF16),
            pltpu.VMEM((waves, npar * HALO, ncol), BF16),
            pltpu.VMEM((waves, npar * HALO, ncol), BF16),
            pltpu.VMEM((8, ncol), F32),
            pltpu.VMEM((8, ncol), F32),
            pltpu.VMEM((gsize * waves, 8, ncol), F32),
            pltpu.VMEM((ngroup, 8, ncol), F32),
            dma((4,)),
            dma((7,)), dma((7,)),
            dma((2, waves)), dma((2, waves)),
            dma((2, waves)), dma((2, waves)),
            dma((2, waves)), dma((2, waves)),
            dma((gsize * waves,)), dma((gsize * waves,)),
            dma((ngroup,)), dma((ngroup,)),
        ],
        compiler_params=pltpu.CompilerParams(
            collective_id=0, has_side_effects=True, vmem_limit_bytes=48 * 1024 * 1024
        ),
    )(
        params, dual_in, jacobian.reshape(images, rows, ncol),
        observed.reshape(nimg, rows, ncol), response, psf,
        step_size.reshape(1), dual_step.reshape(1), tv_bound.reshape(1), clip_bound.reshape(1),
    )
    return state, dual_out, misfit.reshape(())


def solution(mesh):
    in_specs = (
        P(None, "tile", None),
        P(None, None, "tile", None),
        P(None, None, "tile", None),
        P(None, "wave"),
        P(None, "wave", "tile", None),
        P(),
        P(),
        P(),
        P(),
        P(),
    )
    out_specs = (P(None, "tile", None), P(None, None, "tile", None), P())
    return jax.shard_map(
        per_device, mesh=mesh, in_specs=in_specs, out_specs=out_specs, check_vma=False
    )
```

```python
import functools

import jax
import jax.numpy as jnp
from jax import lax
from jax.experimental import pallas as pl
from jax.experimental.pallas import tpu as pltpu
from jax.sharding import PartitionSpec as P

MESH = pl.DeviceIdType.MESH
HALO = 8
EDGE = 2 * HALO
TAPS = 17
PAIRS = 9
F32 = jnp.float32
BF16 = jnp.bfloat16


def split_hi_lo(value):
    high = value.astype(BF16).astype(F32)
    return high, value - high


def group_size(count):
    size = 1
    while size * size < count:
        size *= 2
    return size if count % size == 0 else count


def kernel(
    tiles, waves, total_count,
    params_h, dual_h, jac_h, obs_h, response, psf, step_size, dual_step, tv_bound, clip_bound,
    x_out, d_out, m_out,
    params, dual, jac, obs,
    mats, obs_f, jac_f, terms, pairs, proj, acc, xpad, dpad, base, respad, psfpad, rt, rbf, rtb,
    jac_edge, jac_up, jac_dn, par_up, par_dn, dual_up, div_edge, div_up, div_dn,
    full0, edge0, full1, edge1, full0_in, up0_in, dn0_in, full1_in, up1_in, dn1_in,
    m_own, m_mid, m_group, m_cross,
    local, in_send, in_recv, f_send, f_recv, u_send, u_recv, d_send, d_recv,
    mg_send, mg_recv, mc_send, mc_recv,
):
    npar, rows, ncol = params.shape
    images = jac.shape[0]
    stokes = images // npar
    nwave = response.shape[1]
    nimg = stokes * nwave
    width = -(-images // 8) * 8
    wide = -(-images // 16) * 16
    padded = rows + EDGE
    npair = padded // 2
    opair = rows // 2
    me_t = lax.axis_index("tile")
    me_w = lax.axis_index("wave")
    up = lax.rem(me_t + tiles - 1, tiles)
    down = lax.rem(me_t + 1, tiles)
    gsize = group_size(tiles)
    ngroup = tiles // gsize
    my_group = me_t // gsize
    my_place = lax.rem(me_t, gsize)
    spin = [me_w] + [lax.rem(me_w + d, waves) for d in range(1, waves)]
    group_tiles = [me_t]
    group_tiles += [my_group * gsize + lax.rem(my_place + d, gsize) for d in range(1, gsize)]
    group_peers = [(t, w) for i, t in enumerate(group_tiles) for j, w in enumerate(spin) if i + j > 0]
    cross_peers = [
        (lax.rem(my_group + d, ngroup) * gsize + my_place, me_w) for d in range(1, ngroup)
    ]

    barrier = pltpu.get_barrier_semaphore()
    peers = [(t, w) for w in spin for t in (up, down)] + group_peers + cross_peers
    for peer in peers:
        pl.semaphore_signal(barrier, inc=1, device_id=peer, device_id_type=MESH)
    fetch = [
        pltpu.make_async_copy(jac_h, jac, local.at[0]),
        pltpu.make_async_copy(params_h, params, local.at[1]),
        pltpu.make_async_copy(dual_h, dual, local.at[2]),
        pltpu.make_async_copy(obs_h, obs, local.at[3]),
    ]
    for copy in fetch:
        copy.start()
    fetch[0].wait()
    for m in range(images):
        jac_f[m, HALO:HALO + rows, :] = jac[m].astype(F32)
    jac_edge[0] = jac_f[:, HALO:EDGE, :].reshape(images * HALO, ncol).astype(BF16)
    jac_edge[1] = jac_f[:, rows:rows + HALO, :].reshape(images * HALO, ncol).astype(BF16)
    fetch[1].wait()
    fetch[2].wait()
    pl.semaphore_wait(barrier, len(peers))

    def remote(src, dst, send, recv, peer):
        return pltpu.make_async_remote_copy(
            src_ref=src, dst_ref=dst, send_sem=send, recv_sem=recv,
            device_id=peer, device_id_type=MESH,
        )

    above, below = (up, me_w), (down, me_w)
    first = [
        remote(params.at[:, pl.ds(rows - HALO, HALO)], par_up, in_send.at[0], in_recv.at[0], below),
        remote(params.at[:, pl.ds(0, HALO)], par_dn, in_send.at[1], in_recv.at[1], above),
        remote(dual.at[0, :, pl.ds(rows - HALO, HALO)], dual_up, in_send.at[2], in_recv.at[2], below),
        remote(jac_edge.at[1], jac_up, in_send.at[3], in_recv.at[3], below),
        remote(jac_edge.at[0], jac_dn, in_send.at[4], in_recv.at[4], above),
    ]
    for copy in first:
        copy.start()

    step = step_size[0]
    clip = clip_bound[0]
    bound = tv_bound[0]
    dstep = dual_step[0]

    zero_block = jnp.zeros((ncol, ncol), BF16)
    mats[0, ncol:, 0:ncol] = zero_block
    mats[PAIRS - 1, 0:ncol, ncol:] = zero_block
    psfpad[...] = jnp.zeros_like(psfpad)
    psfpad[0:TAPS, 0:TAPS] = psf[...].astype(F32)
    taps = pltpu.roll(psfpad[...], ncol - HALO, 1)
    for tap in range(TAPS):
        line = jnp.broadcast_to(taps[tap:tap + 1, :], (ncol, ncol))
        block = pltpu.roll(line, 0, 1, stride=1, stride_axis=0).astype(BF16)
        if tap % 2 == 0:
            mats[tap // 2, 0:ncol, 0:ncol] = block
            mats[tap // 2, ncol:, ncol:] = block
        else:
            mats[tap // 2, 0:ncol, ncol:] = block
            mats[tap // 2 + 1, ncol:, 0:ncol] = block

    respad[...] = jnp.zeros_like(respad)
    respad[0:npar, 0:nwave] = response[...]
    rt[...] = jnp.zeros_like(rt)
    spread = respad[...]
    for s in range(stokes):
        shifted = spread if s == 0 else pltpu.roll(spread, s * nwave, 1)
        for part in range(3):
            at = part * width + s * npar
            rt[at:at + npar, :] = shifted[0:npar]
    full = rt[...]
    high, low = split_hi_lo(full)
    place = lax.broadcasted_iota(jnp.int32, full.shape, 0)
    rbf[...] = jnp.where(place < 2 * width, high, low).T.astype(BF16)
    rtb[...] = jnp.concatenate([high[0:width], low[0:width]], axis=0).astype(BF16)

    for m in range(images, width):
        terms[m * padded:(m + 1) * padded, :] = jnp.zeros((padded, ncol), F32)
    d1 = params[...]
    xpad[:, HALO:HALO + rows, :] = d1
    d1 = pltpu.roll(d1, ncol - 1, 2) - d1
    d1 = jnp.clip(dual[1] + dstep * d1, -bound, bound)
    d_out[1] = d1
    fetch[3].wait()
    obs_f[...] = obs[...].astype(F32).reshape(nimg * rows, ncol)

    for copy in first:
        copy.wait()
    xpad[:, 0:HALO, :] = par_up[...]
    xpad[:, HALO + rows:, :] = par_dn[...]
    d0 = xpad[:, HALO + 1:HALO + 1 + rows, :] - xpad[:, HALO:HALO + rows, :]
    d0 = jnp.clip(dual[0] + dstep * d0, -bound, bound)
    d_out[0] = d0
    side = xpad[:, 1:HALO + 1, :] - xpad[:, 0:HALO, :]
    dpad[:, 0:HALO, :] = jnp.clip(dual_up[...] + dstep * side, -bound, bound)
    dpad[:, HALO:, :] = d0
    div = (d0 - dpad[:, HALO - 1:HALO - 1 + rows, :]) + (d1 - pltpu.roll(d1, 1, 2))
    base[:, HALO:HALO + rows, :] = div
    div_edge[0] = div[:, 0:HALO, :]
    div_edge[1] = div[:, rows - HALO:, :]
    copies_v = [
        remote(div_edge.at[1], div_up, in_send.at[5], in_recv.at[5], below),
        remote(div_edge.at[0], div_dn, in_send.at[6], in_recv.at[6], above),
    ]
    for copy in copies_v:
        copy.start()
    jac_f[:, 0:HALO, :] = jac_up[...].astype(F32).reshape(images, HALO, ncol)
    jac_f[:, HALO + rows:, :] = jac_dn[...].astype(F32).reshape(images, HALO, ncol)

    zero_k = jnp.zeros((rbf.shape[1] - 3 * width, 2 * ncol), F32)

    def widen(value):
        if wide == width:
            return value.astype(BF16)
        fill = jnp.zeros((wide - width, value.shape[1]), F32)
        return jnp.concatenate([value, fill], axis=0).astype(BF16)

    for it in range(2):
        for m in range(images):
            terms[m * padded:(m + 1) * padded, :] = jac_f[m] * xpad[m % npar]
        for q in range(npair):
            for i in range(2):
                value = terms[pl.ds(2 * q + i, width, stride=padded), :]
                value = jnp.concatenate(split_hi_lo(value), axis=0).astype(BF16)
                pairs[q * 2 * width:(q + 1) * 2 * width, i * ncol:(i + 1) * ncol] = value
        total = None
        for k in range(PAIRS):
            window = pairs[k * 2 * width:(k + opair) * 2 * width, :]
            part = lax.dot_general(
                window, mats[k], (((1,), (1,)), ((), ())), preferred_element_type=F32
            )
            total = part if total is None else total + part
        loss = jnp.zeros((8, ncol), F32)
        for r in range(opair):
            both = total[r * 2 * width:(r + 1) * 2 * width]
            bhi, blo = split_hi_lo(both[:width] + both[width:])
            stack = jnp.concatenate([bhi, blo, bhi, zero_k], axis=0).astype(BF16)
            blurred = jnp.dot(rbf[...], stack, preferred_element_type=F32)
            halves = []
            for i in range(2):
                target = obs_f[pl.ds(2 * r + i, nimg, stride=rows), :]
                resid = blurred[:, i * ncol:(i + 1) * ncol] - target
                held = jnp.clip(resid, -clip, clip)
                if it == 0:
                    huber = held * (resid - 0.5 * held)
                    loss = loss + jnp.sum(huber.reshape(nimg // 8, 8, ncol), axis=0)
                halves.append(held.astype(BF16))
            weighted = jnp.concatenate(halves, axis=1)
            both = jnp.dot(rtb[...], weighted, preferred_element_type=F32)
            proj[r * wide:(r + 1) * wide, :] = widen(both[:width] + both[width:])
        if it == 0:
            m_own[...] = loss
            slot = my_place * waves + me_w
            m_group[slot] = loss
            copies_g = [
                remote(m_own, m_group.at[slot], mg_send.at[d], mg_recv.at[d], peer)
                for d, peer in enumerate(group_peers)
            ]
            for copy in copies_g:
                copy.start()
        for k in range(PAIRS):
            back = jnp.dot(proj[...], mats[k], preferred_element_type=F32)
            for q in range(opair):
                part = back[q * wide:(q + 1) * wide]
                at = (k + q) * wide
                if k == 0 or q == opair - 1:
                    acc[at:at + wide, :] = part
                else:
                    acc[at:at + wide, :] += part
        for q in range(npair):
            for i in range(2):
                value = acc[q * wide:q * wide + width, i * ncol:(i + 1) * ncol]
                terms[pl.ds(2 * q + i, width, stride=padded), :] = value
        grads = []
        for p in range(npar):
            grad = None
            for s in range(stokes):
                m = s * npar + p
                part = jac_f[m] * terms[m * padded:(m + 1) * padded, :]
                grad = part if grad is None else grad + part
            grads.append(grad)
        reach = EDGE if it == 0 else HALO
        whole = grads if it == 0 else [g[HALO:HALO + rows] for g in grads]
        whole = jnp.concatenate(whole, axis=0).astype(BF16)
        full_out, edge_out = (full0, edge0) if it == 0 else (full1, edge1)
        full_in, up_in, dn_in = (full0_in, up0_in, dn0_in) if it == 0 else (full1_in, up1_in, dn1_in)
        edge_out[0] = jnp.concatenate([g[:reach] for g in grads], axis=0).astype(BF16)
        edge_out[1] = jnp.concatenate([g[padded - reach:] for g in grads], axis=0).astype(BF16)
        full_out[...] = whole
        full_in[me_w] = whole
        copies = []
        for d in range(waves - 1, -1, -1):
            copies += [
                remote(edge_out.at[1], up_in.at[me_w], u_send.at[it, d], u_recv.at[it, d], (down, spin[d])),
                remote(edge_out.at[0], dn_in.at[me_w], d_send.at[it, d], d_recv.at[it, d], (up, spin[d])),
            ]
        for d in range(1, waves):
            copies.append(
                remote(full_out, full_in.at[me_w], f_send.at[it, d], f_recv.at[it, d], (me_t, spin[d]))
            )
        for copy in copies:
            copy.start()
        if it == 0:
            for copy in copies_v:
                copy.wait()
            base[:, 0:HALO, :] = div_up[...]
            base[:, HALO + rows:, :] = div_dn[...]
            base[...] = xpad[...] + step * base[...]
        for copy in copies:
            copy.wait()

        def added(ref, count):
            value = ref[0].astype(F32)
            for w in range(1, waves):
                value = value + ref[w].astype(F32)
            return value.reshape(npar, count, ncol)

        span = padded if it == 0 else rows
        inner = added(full_in, span)
        top = inner[:, :reach] + added(up_in, reach)
        low = inner[:, span - reach:] + added(dn_in, reach)
        if it == 0:
            kept = [base[:, :reach, :] - step * top]
            if span > 2 * reach:
                kept.append(base[:, reach:span - reach, :] - step * inner[:, reach:span - reach])
            kept.append(base[:, span - reach:, :] - step * low)
            mid = base[:, HALO:HALO + rows, :] - xpad[:, HALO:HALO + rows, :]
            at = 0
            for value in kept:
                xpad[:, at:at + value.shape[1], :] = value
                at += value.shape[1]
            base[:, HALO:HALO + rows, :] = xpad[:, HALO:HALO + rows, :] + mid
            for copy in copies_g:
                copy.wait()
            total_m = m_group[0]
            for g in range(1, gsize * waves):
                total_m = total_m + m_group[g]
            m_mid[...] = total_m
            m_cross[my_group] = total_m
            copies_c = [
                remote(m_mid, m_cross.at[my_group], mc_send.at[d], mc_recv.at[d], peer)
                for d, peer in enumerate(cross_peers)
            ]
            for copy in copies_c:
                copy.start()
        else:
            x_out[:, 0:reach, :] = base[:, HALO:HALO + reach, :] - step * top
            if span > 2 * reach:
                x_out[:, reach:span - reach, :] = (
                    base[:, HALO + reach:HALO + span - reach, :] - step * inner[:, reach:span - reach]
                )
            x_out[:, span - reach:, :] = base[:, HALO + span - reach:HALO + span, :] - step * low
            for copy in copies_c:
                copy.wait()
            tot = m_cross[0]
            for g in range(1, ngroup):
                tot = tot + m_cross[g]
            m_out[0] = jnp.sum(tot) / total_count


def per_device(
    params, dual_in, jacobian, response, observed, psf, step_size, dual_step, tv_bound, clip_bound
):
    stokes, nwave, rows, ncol = observed.shape
    npar = params.shape[0]
    nimg = stokes * nwave
    images = stokes * npar
    width = -(-images // 8) * 8
    wide = -(-images // 16) * 16
    kdim = -(-3 * width // 128) * 128
    padded = rows + EDGE
    npair = padded // 2
    opair = rows // 2
    tiles = lax.axis_size("tile")
    waves = lax.axis_size("wave")
    total_count = float(nimg * waves * rows * tiles * ncol)
    gsize = group_size(tiles)
    ngroup = tiles // gsize
    vmem = pl.BlockSpec(memory_space=pltpu.VMEM)
    smem = pl.BlockSpec(memory_space=pltpu.SMEM)
    hbm = pl.BlockSpec(memory_space=pltpu.HBM)
    dma = pltpu.SemaphoreType.DMA
    state, dual_out, misfit = pl.pallas_call(
        functools.partial(kernel, tiles, waves, total_count),
        out_shape=(
            jax.ShapeDtypeStruct((npar, rows, ncol), F32),
            jax.ShapeDtypeStruct((2, npar, rows, ncol), F32),
            jax.ShapeDtypeStruct((1,), F32),
        ),
        in_specs=[hbm] * 4 + [vmem] * 2 + [smem] * 4,
        out_specs=(vmem, vmem, smem),
        scratch_shapes=[
            pltpu.VMEM((npar, rows, ncol), F32),
            pltpu.VMEM((2, npar, rows, ncol), F32),
            pltpu.VMEM((images, rows, ncol), BF16),
            pltpu.VMEM((nimg, rows, ncol), BF16),
            pltpu.VMEM((PAIRS, 2 * ncol, 2 * ncol), BF16),
            pltpu.VMEM((nimg * rows, ncol), F32),
            pltpu.VMEM((images, padded, ncol), F32),
            pltpu.VMEM((width * padded, ncol), F32),
            pltpu.VMEM((npair * 2 * width, 2 * ncol), BF16),
            pltpu.VMEM((opair * wide, 2 * ncol), BF16),
            pltpu.VMEM((npair * wide, 2 * ncol), F32),
            pltpu.VMEM((npar, padded, ncol), F32),
            pltpu.VMEM((npar, rows + HALO, ncol), F32),
            pltpu.VMEM((npar, padded, ncol), F32),
            pltpu.VMEM((-(-npar // 8) * 8, nimg), F32),
            pltpu.VMEM((-(-TAPS // 8) * 8, ncol), F32),
            pltpu.VMEM((kdim, nimg), F32),
            pltpu.VMEM((nimg, kdim), BF16),
            pltpu.VMEM((2 * width, nimg), BF16),
            pltpu.VMEM((2, images * HALO, ncol), BF16),
            pltpu.VMEM((images * HALO, ncol), BF16),
            pltpu.VMEM((images * HALO, ncol), BF16),
            pltpu.VMEM((npar, HALO, ncol), F32),
            pltpu.VMEM((npar, HALO, ncol), F32),
            pltpu.VMEM((npar, HALO, ncol), F32),
            pltpu.VMEM((2, npar, HALO, ncol), F32),
            pltpu.VMEM((npar, HALO, ncol), F32),
            pltpu.VMEM((npar, HALO, ncol), F32),
            pltpu.VMEM((npar * padded, ncol), BF16),
            pltpu.VMEM((2, npar * EDGE, ncol), BF16),
            pltpu.VMEM((npar * rows, ncol), BF16),
            pltpu.VMEM((2, npar * HALO, ncol), BF16),
            pltpu.VMEM((waves, npar * padded, ncol), BF16),
            pltpu.VMEM((waves, npar * EDGE, ncol), BF16),
            pltpu.VMEM((waves, npar * EDGE, ncol), BF16),
            pltpu.VMEM((waves, npar * rows, ncol), BF16),
            pltpu.VMEM((waves, npar * HALO, ncol), BF16),
            pltpu.VMEM((waves, npar * HALO, ncol), BF16),
            pltpu.VMEM((8, ncol), F32),
            pltpu.VMEM((8, ncol), F32),
            pltpu.VMEM((gsize * waves, 8, ncol), F32),
            pltpu.VMEM((ngroup, 8, ncol), F32),
            dma((4,)),
            dma((7,)), dma((7,)),
            dma((2, waves)), dma((2, waves)),
            dma((2, waves)), dma((2, waves)),
            dma((2, waves)), dma((2, waves)),
            dma((gsize * waves,)), dma((gsize * waves,)),
            dma((ngroup,)), dma((ngroup,)),
        ],
        compiler_params=pltpu.CompilerParams(
            collective_id=0, has_side_effects=True, vmem_limit_bytes=66_000_000
        ),
    )(
        params, dual_in, jacobian.reshape(images, rows, ncol),
        observed.reshape(nimg, rows, ncol), response, psf,
        step_size.reshape(1), dual_step.reshape(1), tv_bound.reshape(1), clip_bound.reshape(1),
    )
    return state, dual_out, misfit.reshape(())


def solution(mesh):
    in_specs = (
        P(None, "tile", None),
        P(None, None, "tile", None),
        P(None, None, "tile", None),
        P(None, "wave"),
        P(None, "wave", "tile", None),
        P(),
        P(),
        P(),
        P(),
        P(),
    )
    out_specs = (P(None, "tile", None), P(None, None, "tile", None), P())
    return jax.shard_map(
        per_device, mesh=mesh, in_specs=in_specs, out_specs=out_specs, check_vma=False
    )
```

```python
import functools

import jax
import jax.numpy as jnp
from jax import lax
from jax.experimental import pallas as pl
from jax.experimental.pallas import tpu as pltpu
from jax.sharding import PartitionSpec as P

MESH = pl.DeviceIdType.MESH
HALO = 8
EDGE = 2 * HALO
TAPS = 17
PAIRS = 9
F32 = jnp.float32
BF16 = jnp.bfloat16


def split_hi_lo(value):
    high = value.astype(BF16).astype(F32)
    return high, value - high


def group_size(count):
    size = 1
    while size * size < count:
        size *= 2
    return size if count % size == 0 else count


def kernel(
    tiles, waves, total_count,
    params_h, dual_h, jac_h, obs_h, response, psf, step_size, dual_step, tv_bound, clip_bound,
    x_out, d_out_h, m_out,
    d_out, params, dual, jac, obs,
    mats, obs_f, jac_f, terms, pairs, proj, acc, xpad, dpad, base, respad, psfpad, rt, rbf, rtb,
    jac_edge, jac_up, jac_dn, par_up, par_dn, dual_up, div_edge, div_up, div_dn,
    full0, edge0, full1, edge1, full0_in, up0_in, dn0_in, full1_in, up1_in, dn1_in,
    m_own, m_mid, m_group, m_cross,
    local, in_send, in_recv, f_send, f_recv, u_send, u_recv, d_send, d_recv,
    mg_send, mg_recv, mc_send, mc_recv,
):
    npar, rows, ncol = params.shape
    images = jac.shape[0]
    stokes = images // npar
    nwave = response.shape[1]
    nimg = stokes * nwave
    width = -(-images // 8) * 8
    wide = -(-images // 16) * 16
    padded = rows + EDGE
    npair = padded // 2
    opair = rows // 2
    me_t = lax.axis_index("tile")
    me_w = lax.axis_index("wave")
    up = lax.rem(me_t + tiles - 1, tiles)
    down = lax.rem(me_t + 1, tiles)
    gsize = group_size(tiles)
    ngroup = tiles // gsize
    my_group = me_t // gsize
    my_place = lax.rem(me_t, gsize)
    spin = [me_w] + [lax.rem(me_w + d, waves) for d in range(1, waves)]
    group_tiles = [me_t]
    group_tiles += [my_group * gsize + lax.rem(my_place + d, gsize) for d in range(1, gsize)]
    group_peers = [(t, w) for i, t in enumerate(group_tiles) for j, w in enumerate(spin) if i + j > 0]
    cross_peers = [
        (lax.rem(my_group + d, ngroup) * gsize + my_place, me_w) for d in range(1, ngroup)
    ]

    barrier = pltpu.get_barrier_semaphore()
    peers = [(t, w) for w in spin for t in (up, down)] + group_peers + cross_peers
    for peer in peers:
        pl.semaphore_signal(barrier, inc=1, device_id=peer, device_id_type=MESH)
    fetch = [
        pltpu.make_async_copy(jac_h, jac, local.at[0]),
        pltpu.make_async_copy(params_h, params, local.at[1]),
        pltpu.make_async_copy(dual_h, dual, local.at[2]),
        pltpu.make_async_copy(obs_h, obs, local.at[3]),
    ]
    for copy in fetch:
        copy.start()
    fetch[0].wait()
    for m in range(images):
        jac_f[m, HALO:HALO + rows, :] = jac[m].astype(F32)
    jac_edge[0] = jac_f[:, HALO:EDGE, :].reshape(images * HALO, ncol).astype(BF16)
    jac_edge[1] = jac_f[:, rows:rows + HALO, :].reshape(images * HALO, ncol).astype(BF16)
    fetch[1].wait()
    fetch[2].wait()
    pl.semaphore_wait(barrier, len(peers))

    def remote(src, dst, send, recv, peer):
        return pltpu.make_async_remote_copy(
            src_ref=src, dst_ref=dst, send_sem=send, recv_sem=recv,
            device_id=peer, device_id_type=MESH,
        )

    above, below = (up, me_w), (down, me_w)
    first = [
        remote(params.at[:, pl.ds(rows - HALO, HALO)], par_up, in_send.at[0], in_recv.at[0], below),
        remote(params.at[:, pl.ds(0, HALO)], par_dn, in_send.at[1], in_recv.at[1], above),
        remote(dual.at[0, :, pl.ds(rows - HALO, HALO)], dual_up, in_send.at[2], in_recv.at[2], below),
        remote(jac_edge.at[1], jac_up, in_send.at[3], in_recv.at[3], below),
        remote(jac_edge.at[0], jac_dn, in_send.at[4], in_recv.at[4], above),
    ]
    for copy in first:
        copy.start()

    step = step_size[0]
    clip = clip_bound[0]
    bound = tv_bound[0]
    dstep = dual_step[0]

    zero_block = jnp.zeros((ncol, ncol), BF16)
    mats[0, ncol:, 0:ncol] = zero_block
    mats[PAIRS - 1, 0:ncol, ncol:] = zero_block
    psfpad[...] = jnp.zeros_like(psfpad)
    psfpad[0:TAPS, 0:TAPS] = psf[...].astype(F32)
    taps = pltpu.roll(psfpad[...], ncol - HALO, 1)
    for tap in range(TAPS):
        line = jnp.broadcast_to(taps[tap:tap + 1, :], (ncol, ncol))
        block = pltpu.roll(line, 0, 1, stride=1, stride_axis=0).astype(BF16)
        if tap % 2 == 0:
            mats[tap // 2, 0:ncol, 0:ncol] = block
            mats[tap // 2, ncol:, ncol:] = block
        else:
            mats[tap // 2, 0:ncol, ncol:] = block
            mats[tap // 2 + 1, ncol:, 0:ncol] = block

    respad[...] = jnp.zeros_like(respad)
    respad[0:npar, 0:nwave] = response[...]
    rt[...] = jnp.zeros_like(rt)
    spread = respad[...]
    for s in range(stokes):
        shifted = spread if s == 0 else pltpu.roll(spread, s * nwave, 1)
        for part in range(3):
            at = part * width + s * npar
            rt[at:at + npar, :] = shifted[0:npar]
    full = rt[...]
    high, low = split_hi_lo(full)
    place = lax.broadcasted_iota(jnp.int32, full.shape, 0)
    rbf[...] = jnp.where(place < 2 * width, high, low).T.astype(BF16)
    rtb[...] = jnp.concatenate([high[0:width], low[0:width]], axis=0).astype(BF16)

    for m in range(images, width):
        terms[m * padded:(m + 1) * padded, :] = jnp.zeros((padded, ncol), F32)
    d1 = params[...]
    xpad[:, HALO:HALO + rows, :] = d1
    d1 = pltpu.roll(d1, ncol - 1, 2) - d1
    d1 = jnp.clip(dual[1] + dstep * d1, -bound, bound)
    d_out[1] = d1
    fetch[3].wait()
    obs_f[...] = obs[...].astype(F32).reshape(nimg * rows, ncol)

    for copy in first:
        copy.wait()
    xpad[:, 0:HALO, :] = par_up[...]
    xpad[:, HALO + rows:, :] = par_dn[...]
    d0 = xpad[:, HALO + 1:HALO + 1 + rows, :] - xpad[:, HALO:HALO + rows, :]
    d0 = jnp.clip(dual[0] + dstep * d0, -bound, bound)
    d_out[0] = d0
    side = xpad[:, 1:HALO + 1, :] - xpad[:, 0:HALO, :]
    dpad[:, 0:HALO, :] = jnp.clip(dual_up[...] + dstep * side, -bound, bound)
    dpad[:, HALO:, :] = d0
    div = (d0 - dpad[:, HALO - 1:HALO - 1 + rows, :]) + (d1 - pltpu.roll(d1, 1, 2))
    base[:, HALO:HALO + rows, :] = div
    div_edge[0] = div[:, 0:HALO, :]
    div_edge[1] = div[:, rows - HALO:, :]
    copies_v = [
        remote(div_edge.at[1], div_up, in_send.at[5], in_recv.at[5], below),
        remote(div_edge.at[0], div_dn, in_send.at[6], in_recv.at[6], above),
    ]
    for copy in copies_v:
        copy.start()
    jac_f[:, 0:HALO, :] = jac_up[...].astype(F32).reshape(images, HALO, ncol)
    jac_f[:, HALO + rows:, :] = jac_dn[...].astype(F32).reshape(images, HALO, ncol)

    keep = pltpu.make_async_copy(d_out, d_out_h, local.at[4])
    keep.start()
    zero_k = jnp.zeros((rbf.shape[1] - 3 * width, 2 * ncol), F32)

    def widen(value):
        if wide == width:
            return value.astype(BF16)
        fill = jnp.zeros((wide - width, value.shape[1]), F32)
        return jnp.concatenate([value, fill], axis=0).astype(BF16)

    for it in range(2):
        for m in range(images):
            terms[m * padded:(m + 1) * padded, :] = jac_f[m] * xpad[m % npar]
        for q in range(npair):
            for i in range(2):
                value = terms[pl.ds(2 * q + i, width, stride=padded), :]
                value = jnp.concatenate(split_hi_lo(value), axis=0).astype(BF16)
                pairs[q * 2 * width:(q + 1) * 2 * width, i * ncol:(i + 1) * ncol] = value
        total = None
        for k in range(PAIRS):
            window = pairs[k * 2 * width:(k + opair) * 2 * width, :]
            part = lax.dot_general(
                window, mats[k], (((1,), (1,)), ((), ())), preferred_element_type=F32
            )
            total = part if total is None else total + part
        loss = jnp.zeros((8, ncol), F32)
        for r in range(opair):
            both = total[r * 2 * width:(r + 1) * 2 * width]
            bhi, blo = split_hi_lo(both[:width] + both[width:])
            stack = jnp.concatenate([bhi, blo, bhi, zero_k], axis=0).astype(BF16)
            blurred = jnp.dot(rbf[...], stack, preferred_element_type=F32)
            halves = []
            for i in range(2):
                target = obs_f[pl.ds(2 * r + i, nimg, stride=rows), :]
                resid = blurred[:, i * ncol:(i + 1) * ncol] - target
                held = jnp.clip(resid, -clip, clip)
                if it == 0:
                    huber = held * (resid - 0.5 * held)
                    loss = loss + jnp.sum(huber.reshape(nimg // 8, 8, ncol), axis=0)
                halves.append(held.astype(BF16))
            weighted = jnp.concatenate(halves, axis=1)
            both = jnp.dot(rtb[...], weighted, preferred_element_type=F32)
            proj[r * wide:(r + 1) * wide, :] = widen(both[:width] + both[width:])
        if it == 0:
            m_own[...] = loss
            slot = my_place * waves + me_w
            m_group[slot] = loss
            copies_g = [
                remote(m_own, m_group.at[slot], mg_send.at[d], mg_recv.at[d], peer)
                for d, peer in enumerate(group_peers)
            ]
            for copy in copies_g:
                copy.start()
        for k in range(PAIRS):
            back = jnp.dot(proj[...], mats[k], preferred_element_type=F32)
            for q in range(opair):
                part = back[q * wide:(q + 1) * wide]
                at = (k + q) * wide
                if k == 0 or q == opair - 1:
                    acc[at:at + wide, :] = part
                else:
                    acc[at:at + wide, :] += part
        for q in range(npair):
            for i in range(2):
                value = acc[q * wide:q * wide + width, i * ncol:(i + 1) * ncol]
                terms[pl.ds(2 * q + i, width, stride=padded), :] = value
        grads = []
        for p in range(npar):
            grad = None
            for s in range(stokes):
                m = s * npar + p
                part = jac_f[m] * terms[m * padded:(m + 1) * padded, :]
                grad = part if grad is None else grad + part
            grads.append(grad)
        reach = EDGE if it == 0 else HALO
        whole = grads if it == 0 else [g[HALO:HALO + rows] for g in grads]
        whole = jnp.concatenate(whole, axis=0).astype(BF16)
        full_out, edge_out = (full0, edge0) if it == 0 else (full1, edge1)
        full_in, up_in, dn_in = (full0_in, up0_in, dn0_in) if it == 0 else (full1_in, up1_in, dn1_in)
        edge_out[0] = jnp.concatenate([g[:reach] for g in grads], axis=0).astype(BF16)
        edge_out[1] = jnp.concatenate([g[padded - reach:] for g in grads], axis=0).astype(BF16)
        full_out[...] = whole
        full_in[me_w] = whole
        copies = []
        for d in range(waves - 1, -1, -1):
            copies += [
                remote(edge_out.at[1], up_in.at[me_w], u_send.at[it, d], u_recv.at[it, d], (down, spin[d])),
                remote(edge_out.at[0], dn_in.at[me_w], d_send.at[it, d], d_recv.at[it, d], (up, spin[d])),
            ]
        for d in range(1, waves):
            copies.append(
                remote(full_out, full_in.at[me_w], f_send.at[it, d], f_recv.at[it, d], (me_t, spin[d]))
            )
        for copy in copies:
            copy.start()
        if it == 0:
            for copy in copies_v:
                copy.wait()
            base[:, 0:HALO, :] = div_up[...]
            base[:, HALO + rows:, :] = div_dn[...]
            base[...] = xpad[...] + step * base[...]
        for copy in copies:
            copy.wait()

        def added(ref, count):
            value = ref[0].astype(F32)
            for w in range(1, waves):
                value = value + ref[w].astype(F32)
            return value.reshape(npar, count, ncol)

        span = padded if it == 0 else rows
        inner = added(full_in, span)
        top = inner[:, :reach] + added(up_in, reach)
        low = inner[:, span - reach:] + added(dn_in, reach)
        if it == 0:
            kept = [base[:, :reach, :] - step * top]
            if span > 2 * reach:
                kept.append(base[:, reach:span - reach, :] - step * inner[:, reach:span - reach])
            kept.append(base[:, span - reach:, :] - step * low)
            mid = base[:, HALO:HALO + rows, :] - xpad[:, HALO:HALO + rows, :]
            at = 0
            for value in kept:
                xpad[:, at:at + value.shape[1], :] = value
                at += value.shape[1]
            base[:, HALO:HALO + rows, :] = xpad[:, HALO:HALO + rows, :] + mid
            for copy in copies_g:
                copy.wait()
            total_m = m_group[0]
            for g in range(1, gsize * waves):
                total_m = total_m + m_group[g]
            m_mid[...] = total_m
            m_cross[my_group] = total_m
            copies_c = [
                remote(m_mid, m_cross.at[my_group], mc_send.at[d], mc_recv.at[d], peer)
                for d, peer in enumerate(cross_peers)
            ]
            for copy in copies_c:
                copy.start()
        else:
            x_out[:, 0:reach, :] = base[:, HALO:HALO + reach, :] - step * top
            if span > 2 * reach:
                x_out[:, reach:span - reach, :] = (
                    base[:, HALO + reach:HALO + span - reach, :] - step * inner[:, reach:span - reach]
                )
            x_out[:, span - reach:, :] = base[:, HALO + span - reach:HALO + span, :] - step * low
            for copy in copies_c + [keep]:
                copy.wait()
            tot = m_cross[0]
            for g in range(1, ngroup):
                tot = tot + m_cross[g]
            m_out[0] = jnp.sum(tot) / total_count


def per_device(
    params, dual_in, jacobian, response, observed, psf, step_size, dual_step, tv_bound, clip_bound
):
    stokes, nwave, rows, ncol = observed.shape
    npar = params.shape[0]
    nimg = stokes * nwave
    images = stokes * npar
    width = -(-images // 8) * 8
    wide = -(-images // 16) * 16
    kdim = -(-3 * width // 128) * 128
    padded = rows + EDGE
    npair = padded // 2
    opair = rows // 2
    tiles = lax.axis_size("tile")
    waves = lax.axis_size("wave")
    total_count = float(nimg * waves * rows * tiles * ncol)
    gsize = group_size(tiles)
    ngroup = tiles // gsize
    vmem = pl.BlockSpec(memory_space=pltpu.VMEM)
    smem = pl.BlockSpec(memory_space=pltpu.SMEM)
    hbm = pl.BlockSpec(memory_space=pltpu.HBM)
    dma = pltpu.SemaphoreType.DMA
    state, dual_out, misfit = pl.pallas_call(
        functools.partial(kernel, tiles, waves, total_count),
        out_shape=(
            jax.ShapeDtypeStruct((npar, rows, ncol), F32),
            jax.ShapeDtypeStruct((2, npar, rows, ncol), F32),
            jax.ShapeDtypeStruct((1,), F32),
        ),
        in_specs=[hbm] * 4 + [vmem] * 2 + [smem] * 4,
        out_specs=(vmem, hbm, smem),
        scratch_shapes=[
            pltpu.VMEM((2, npar, rows, ncol), F32),
            pltpu.VMEM((npar, rows, ncol), F32),
            pltpu.VMEM((2, npar, rows, ncol), F32),
            pltpu.VMEM((images, rows, ncol), BF16),
            pltpu.VMEM((nimg, rows, ncol), BF16),
            pltpu.VMEM((PAIRS, 2 * ncol, 2 * ncol), BF16),
            pltpu.VMEM((nimg * rows, ncol), F32),
            pltpu.VMEM((images, padded, ncol), F32),
            pltpu.VMEM((width * padded, ncol), F32),
            pltpu.VMEM((npair * 2 * width, 2 * ncol), BF16),
            pltpu.VMEM((opair * wide, 2 * ncol), BF16),
            pltpu.VMEM((npair * wide, 2 * ncol), F32),
            pltpu.VMEM((npar, padded, ncol), F32),
            pltpu.VMEM((npar, rows + HALO, ncol), F32),
            pltpu.VMEM((npar, padded, ncol), F32),
            pltpu.VMEM((-(-npar // 8) * 8, nimg), F32),
            pltpu.VMEM((-(-TAPS // 8) * 8, ncol), F32),
            pltpu.VMEM((kdim, nimg), F32),
            pltpu.VMEM((nimg, kdim), BF16),
            pltpu.VMEM((2 * width, nimg), BF16),
            pltpu.VMEM((2, images * HALO, ncol), BF16),
            pltpu.VMEM((images * HALO, ncol), BF16),
            pltpu.VMEM((images * HALO, ncol), BF16),
            pltpu.VMEM((npar, HALO, ncol), F32),
            pltpu.VMEM((npar, HALO, ncol), F32),
            pltpu.VMEM((npar, HALO, ncol), F32),
            pltpu.VMEM((2, npar, HALO, ncol), F32),
            pltpu.VMEM((npar, HALO, ncol), F32),
            pltpu.VMEM((npar, HALO, ncol), F32),
            pltpu.VMEM((npar * padded, ncol), BF16),
            pltpu.VMEM((2, npar * EDGE, ncol), BF16),
            pltpu.VMEM((npar * rows, ncol), BF16),
            pltpu.VMEM((2, npar * HALO, ncol), BF16),
            pltpu.VMEM((waves, npar * padded, ncol), BF16),
            pltpu.VMEM((waves, npar * EDGE, ncol), BF16),
            pltpu.VMEM((waves, npar * EDGE, ncol), BF16),
            pltpu.VMEM((waves, npar * rows, ncol), BF16),
            pltpu.VMEM((waves, npar * HALO, ncol), BF16),
            pltpu.VMEM((waves, npar * HALO, ncol), BF16),
            pltpu.VMEM((8, ncol), F32),
            pltpu.VMEM((8, ncol), F32),
            pltpu.VMEM((gsize * waves, 8, ncol), F32),
            pltpu.VMEM((ngroup, 8, ncol), F32),
            dma((5,)),
            dma((7,)), dma((7,)),
            dma((2, waves)), dma((2, waves)),
            dma((2, waves)), dma((2, waves)),
            dma((2, waves)), dma((2, waves)),
            dma((gsize * waves,)), dma((gsize * waves,)),
            dma((ngroup,)), dma((ngroup,)),
        ],
        compiler_params=pltpu.CompilerParams(
            collective_id=0, has_side_effects=True, vmem_limit_bytes=66_000_000
        ),
    )(
        params, dual_in, jacobian.reshape(images, rows, ncol),
        observed.reshape(nimg, rows, ncol), response, psf,
        step_size.reshape(1), dual_step.reshape(1), tv_bound.reshape(1), clip_bound.reshape(1),
    )
    return state, dual_out, misfit.reshape(())


def solution(mesh):
    in_specs = (
        P(None, "tile", None),
        P(None, None, "tile", None),
        P(None, None, "tile", None),
        P(None, "wave"),
        P(None, "wave", "tile", None),
        P(),
        P(),
        P(),
        P(),
        P(),
    )
    out_specs = (P(None, "tile", None), P(None, None, "tile", None), P())
    return jax.shard_map(
        per_device, mesh=mesh, in_specs=in_specs, out_specs=out_specs, check_vma=False
    )
```
